512 devices in a mesh: dp: 8 (over z_lo, core), basis: 64 (over z_hi, y, x).
Axes of the slice: x: 4, y: 8, z: 8 (z_hi: 2, z_lo: 4; z = z_hi * 4 + z_lo), core: 2. Of those that a mesh axis runs over, the one named last changes fastest.
Arguments:
- train_inputs: bfloat16 [8192, 8192], P('dp', 'basis'), may hold values from -6 to 6
- out_grads: bfloat16 [8192, 28672], P('dp', 'basis'), may hold values from -0.09375 to 0.09375
- basis_in: bfloat16 [8192, 128], P('basis'), may hold values from -0.0625 to 0.0625
- basis_out: bfloat16 [28672, 512], P('basis'), may hold values from -0.03125 to 0.03125
- query_left: bfloat16 [8192, 512], P('basis'), may hold values from -0.09375 to 0.09375
- query_right: bfloat16 [28672, 512], P('basis'), may hold values from -0.09375 to 0.09375
- eigenvalues: float32 [128, 512], P(None, 'basis'), may hold values from 0.2 to 4
Outputs:
- scores: float32 [8, 16], P('dp')
- damped_gradient: float32 [8, 128, 512], P('dp', None, 'basis')
The draws below stay inside these ranges and needn't reach their ends.
All inputs are finite; a program needn't handle non-finite values.
Results may differ from the reference program's by a relative error of at most 0.003.
Values may be sent and summed in bfloat16 or wider, within the bound.
No kernel may reach another device: no remote copies, remote signals or barrier semaphores. Data moves between devices by JAX's collectives and lax.ppermute only.
A program may use at most 64 MiB of HBM per device.

```python
import math
import jax
import jax.numpy as jnp
from jax import lax

DI = 8192
DO = 28672
EA = 128
ES = 512
Q = 16
R = 32
TOK_SEQ = 1024
TOKENS = 8192
N_DP = 8


def steps_of(stream_key, dims, split, low, top_value):
    gain = 1.0
    for dim, shards_of in split:
        draws = jax.random.uniform(jax.random.fold_in(jax.random.fold_in(stream_key, 6), dim), (shards_of,), jnp.float32, low / len(split), top_value / len(split))
        gain = gain * jnp.repeat(jnp.exp(draws), dims[dim] // shards_of).reshape((-1,) + (1,) * (len(dims) - 1 - dim))
    return gain


def scatter_about(key, extent, width, limit, split=(), held_as=jnp.bfloat16):
    gain = steps_of(key, extent, split, -0.22, 0.18) if split else 1.0
    array = jax.random.normal(key, extent, jnp.float32) * width * gain
    return jnp.minimum(jnp.maximum(array, -limit), limit).astype(held_as)


def setup_inputs(seed: int = 0) -> dict:
    splits = jax.random.split(jax.random.key(seed), 8)
    return {
        "train_inputs": scatter_about(splits[0], (TOKENS, DI), 1.0, 6.0, ((0, 8), (1, 64))),
        "out_grads": scatter_about(splits[1], (TOKENS, DO), 0.015625, 0.09375, ((0, 8), (1, 64))),
        "basis_in": scatter_about(splits[2], (DI, EA), DI ** -0.5, 0.0625, ((0, 64),)),
        "basis_out": scatter_about(splits[3], (DO, ES), DO ** -0.5, 0.03125, ((0, 64),)),
        "query_left": scatter_about(splits[4], (DI, Q * R), 0.015625, 0.09375, ((0, 64),)),
        "query_right": scatter_about(splits[5], (DO, Q * R), 0.015625, 0.09375, ((0, 64),)),
        "eigenvalues": jnp.clip(jnp.exp(math.log(4.0) - 2.9957323 * jax.random.uniform(splits[6], (EA, ES), jnp.float32) ** steps_of(splits[6], (EA, ES), ((1, 64),), -0.2, 0.2)), 0.2, 4.0),
    }


damping = 0.1


def reference(train_inputs, out_grads, basis_in, basis_out, query_left, query_right, eigenvalues):
    left_rot = jnp.dot(basis_in.T, query_left, preferred_element_type=jnp.float32)
    right_rot = jnp.dot(query_right.T, basis_out, preferred_element_type=jnp.float32)
    basis_wide = basis_out.astype(jnp.float32)
    score_rows = []
    damped_rows = []
    for seq in range(N_DP):
        inputs_seq = train_inputs[seq * TOK_SEQ:(seq + 1) * TOK_SEQ]
        grads_seq = out_grads[seq * TOK_SEQ:(seq + 1) * TOK_SEQ]
        proj = jnp.dot(inputs_seq, basis_in, preferred_element_type=jnp.float32).astype(jnp.bfloat16)
        moment = jnp.dot(proj.T, grads_seq, preferred_element_type=jnp.float32)
        rotated = jnp.dot(moment, basis_wide, precision=lax.Precision.HIGHEST)
        damped = rotated / (eigenvalues + damping)
        coupled = jnp.dot(damped, right_rot.T, precision=lax.Precision.HIGHEST)
        per_query = jnp.sum((left_rot * coupled).reshape(EA, Q, R), axis=(0, 2))
        score_rows.append(per_query)
        damped_rows.append(damped)
    return jnp.stack(score_rows), jnp.stack(damped_rows)
```

```python
import jax
import jax.numpy as jnp
from jax import lax
from jax.experimental import pallas as pl
from jax.experimental.pallas import tpu as pltpu
from jax.sharding import Mesh, PartitionSpec as P

F32 = jnp.float32
BF16 = jnp.bfloat16
damping = 0.1

PLANE = ("y", "x")
COLUMN = ("dp", "zh")
N = 32


def tn(a, b):
    return lax.dot_general(a, b, (((0,), (0,)), ((), ())), preferred_element_type=F32)


def call(kernel, out_shape, *args):
    return pl.pallas_call(
        kernel,
        out_shape=out_shape,
        compiler_params=pltpu.CompilerParams(vmem_limit_bytes=12 * 1024 * 1024),
    )(*args)


def partials(x_ref, bi_ref, ql_ref, bo_ref, qr_ref, o_ref):
    dp = lax.axis_index("dp")
    block = pl.ds(pl.multiple_of((dp // 2) * 128, 128), 128)
    half = pl.ds(pl.multiple_of((dp % 2) * 256, 128), 256)
    proj = jnp.dot(x_ref[...], bi_ref[...], preferred_element_type=F32)
    o_ref[:, 0:32, :] = proj.reshape(N, 32, 128)
    right = tn(bo_ref[:, half], qr_ref[:, block])
    o_ref[:, 32:40, :] = right.reshape(N, 8, 128)
    left = tn(ql_ref[:, block], bi_ref[...]).reshape(N // 2, 1, 8, 128)
    o_ref[:, 40:48, :] = jnp.broadcast_to(left, (N // 2, 2, 8, 128)).reshape(N, 8, 128)


def plane_sum(r_ref, eig_ref, o_ref):
    o_ref[0:48] = jnp.sum(r_ref[...], axis=0)
    o_ref[48:56] = eig_ref[...]


def finish(a_ref, b_ref, o_ref, right_ref, eig_ref):
    total = a_ref[0:48] + b_ref[0:48]
    left = total[40:48]
    high = left.astype(BF16).astype(F32)
    odd = lax.axis_index("x") % 2 == 1
    piece = jnp.where(odd, left - high, high).astype(BF16)
    o_ref[:, 0:32, :] = jnp.broadcast_to(total[0:32].astype(BF16)[None], (N, 32, 128))
    o_ref[:, 32:40, :] = jnp.broadcast_to(piece[None], (N, 8, 128))
    right_ref[...] = total[32:40]
    first = lax.axis_index("zh") == 0
    eig_ref[0:8] = jnp.where(first, a_ref[48:56], b_ref[48:56])
    eig_ref[8:16] = jnp.where(first, b_ref[48:56], a_ref[48:56])


def rotate(r_ref, g_ref, bo_ref, right_ref, o_ref, w_ref):
    proj = r_ref[:, 0:32, :].reshape(N * 32, 128)
    moment = jnp.dot(g_ref[...], proj, preferred_element_type=F32)
    m1 = moment.astype(BF16)
    rest = moment - m1.astype(F32)
    m2 = rest.astype(BF16)
    m3 = (rest - m2.astype(F32)).astype(BF16)
    bo = bo_ref[...]
    rotated = (tn(bo, m3) + tn(bo, m2)) + tn(bo, m1)
    o_ref[:, 0:8, :] = rotated[0:256].reshape(N, 8, 128)
    o_ref[:, 8:16, :] = rotated[256:512].reshape(N, 8, 128)
    pieces = r_ref[:, 32:40, :].astype(F32).reshape(N // 2, 2, 8, 128)
    left = (pieces[:, 0] + pieces[:, 1]).reshape(128, 128)
    right = right_ref[...]
    rows = jnp.concatenate([right, right, right, right], axis=0)
    query = lax.broadcasted_iota(jnp.int32, (32, 128), 0) // 8
    column = lax.broadcasted_iota(jnp.int32, (32, 128), 1) // 32
    rows = jnp.where(query == column, rows, 0.0)
    w_ref[...] = jnp.dot(rows, left, precision=lax.Precision.HIGHEST, preferred_element_type=F32)


def column_pack(r_ref, w_ref, o_ref, s_ref):
    total = jnp.sum(r_ref[...], axis=0)
    zh = lax.axis_index("zh")
    mine = w_ref[pl.ds(pl.multiple_of(zh * 16, 16), 16)]
    o_ref[...] = jnp.broadcast_to(mine[None], (16, 16, 128))
    o_ref[2 * lax.axis_index("dp") + 1 - zh] = total
    s_ref[...] = total


def score(r_ref, s_ref, w_ref, eig_ref, d_ref, o_ref):
    zh = lax.axis_index("zh")
    partner = 2 * lax.axis_index("dp") + 1 - zh
    damped = (s_ref[...] + r_ref[partner]) / (eig_ref[...] + damping)
    d_ref[...] = jnp.where(zh == 0, damped[0:8], damped[8:16])
    local = w_ref[pl.ds(pl.multiple_of((1 - zh) * 16, 16), 16)]

    def weights(source, rows):
        return jnp.where(partner == source, local[rows], r_ref[source, rows])

    sums = []
    for q in range(16):
        rows = slice((q % 2) * 8, (q % 2) * 8 + 8)
        even = 4 * (q // 4) + (q % 4) // 2
        part = weights(even, rows) * damped[0:8] + weights(even + 2, rows) * damped[8:16]
        sums.append(jnp.sum(part, axis=0, keepdims=True))
    sums = jnp.concatenate(sums, axis=0)
    ones = jnp.ones((8, 128), F32)
    row = lax.dot_general(ones, jnp.concatenate([sums, jnp.zeros((112, 128), F32)], axis=0),
                          (((1,), (1,)), ((), ())), precision=lax.Precision.HIGHEST, preferred_element_type=F32)
    o_ref[...] = jnp.broadcast_to(row[None], (N, 8, 128))


def last_sum(r_ref, o_ref):
    o_ref[...] = jnp.sum(r_ref[...], axis=0)[0:1, 0:16]


def on_device(train_inputs, out_grads, basis_in, basis_out, query_left, query_right, eigenvalues):
    def shape(*dims, dtype=F32):
        return jax.ShapeDtypeStruct(dims, dtype)

    part = call(partials, shape(N, 48, 128), train_inputs, basis_in, query_left, basis_out, query_right)
    part = lax.all_to_all(part, PLANE, 0, 0, tiled=True)
    mine = call(plane_sum, shape(56, 128), part, eigenvalues.T)
    other = lax.ppermute(mine, "zh", [(0, 1), (1, 0)])
    full, right, eig = call(
        finish, (shape(N, 40, 128, dtype=BF16), shape(8, 128), shape(16, 128)), mine, other)
    full = lax.all_to_all(full, PLANE, 0, 0, tiled=True)
    rotated, weights = call(
        rotate, (shape(N, 16, 128), shape(32, 128)), full, out_grads.T, basis_out, right)
    rotated = lax.all_to_all(rotated, PLANE, 0, 0, tiled=True)
    packed, half = call(column_pack, (shape(16, 16, 128), shape(16, 128)), rotated, weights)
    packed = lax.all_to_all(packed, COLUMN, 0, 0, tiled=True)
    damped, scores = call(score, (shape(8, 128), shape(N, 8, 128)), packed, half, weights, eig)
    scores = lax.all_to_all(scores, PLANE, 0, 0, tiled=True)
    scores = call(last_sum, shape(1, 16), scores)
    return scores, damped.T[None]


def solution(mesh):
    fine = Mesh(mesh.devices.reshape(8, 2, 8, 4), ("dp", "zh", "y", "x"))
    basis = ("zh", "y", "x")
    in_specs = (
        P("dp", basis),
        P("dp", basis),
        P(basis, None),
        P(basis, None),
        P(basis, None),
        P(basis, None),
        P(None, basis),
    )
    out_specs = (P("dp", None), P("dp", None, basis))
    return jax.shard_map(
        on_device, mesh=fine, in_specs=in_specs, out_specs=out_specs, check_vma=False
    )
```

```python
import jax
import jax.numpy as jnp
from jax import lax
from jax.experimental import pallas as pl
from jax.experimental.pallas import tpu as pltpu
from jax.sharding import Mesh, PartitionSpec as P

F32 = jnp.float32
BF16 = jnp.bfloat16
damping = 0.1

PLANE = ("y", "x")
COLUMN = ("dp", "zh")
N = 32


def tn(a, b):
    return lax.dot_general(a, b, (((0,), (0,)), ((), ())), preferred_element_type=F32)


def call(kernel, out_shape, *args):
    return pl.pallas_call(
        kernel,
        out_shape=out_shape,
        compiler_params=pltpu.CompilerParams(vmem_limit_bytes=12 * 1024 * 1024),
    )(*args)


def split(value):
    high = value.astype(BF16).astype(F32)
    return high, value - high


def partials(x_hbm, bi_hbm, ql_hbm, bo_hbm, qr_hbm, o_ref, x_ref, bi_ref, ql_ref, bo_ref, qr_ref, sem):
    dp = lax.axis_index("dp")
    block = pl.ds(pl.multiple_of((dp // 2) * 128, 128), 128)
    half = pl.ds(pl.multiple_of((dp % 2) * 256, 128), 256)
    moves = [
        (bi_hbm, bi_ref), (x_hbm, x_ref), (ql_hbm.at[:, block], ql_ref),
        (qr_hbm.at[:, block], qr_ref), (bo_hbm.at[:, half], bo_ref),
    ]
    moves = [pltpu.make_async_copy(src, dst, sem.at[k]) for k, (src, dst) in enumerate(moves)]
    for move in moves:
        move.start()
    moves[0].wait()
    moves[1].wait()
    proj = jnp.dot(x_ref[...], bi_ref[...], preferred_element_type=F32)
    high, low = split(proj)
    o_ref[:, 0:32, :] = high.astype(BF16).reshape(N, 32, 128)
    o_ref[:, 32:64, :] = low.astype(BF16).reshape(N, 32, 128)
    moves[2].wait()
    high, low = split(tn(ql_ref[...], bi_ref[...]).reshape(N // 2, 8, 128))
    top = lax.broadcasted_iota(jnp.int32, (N // 2, 8, 128), 1) < 4
    even = jnp.where(top, high, jnp.roll(low, 4, axis=1))
    odd = jnp.where(top, jnp.roll(high, 4, axis=1), low)
    left = jnp.concatenate([even[:, None], odd[:, None]], axis=1).reshape(N, 8, 128)
    moves[3].wait()
    moves[4].wait()
    high, low = split(tn(bo_ref[...], qr_ref[...]).reshape(N, 8, 128))
    o_ref[:, 64:88, :] = jnp.concatenate([high, low, left], axis=1).astype(BF16)


def plane_sum(r_ref, eig_ref, o_ref):
    total = jnp.sum(r_ref[...].astype(F32), axis=0)
    o_ref[0:32] = total[0:32] + total[32:64]
    o_ref[32:40] = total[64:72] + total[72:80]
    o_ref[40:48] = total[80:88]
    o_ref[48:56] = eig_ref[...]


def finish(a_ref, b_ref, o_ref, right_ref, eig_ref):
    total = a_ref[0:48] + b_ref[0:48]
    left = total[40:48] + jnp.roll(total[40:48], 4, axis=0)
    high, low = split(left)
    piece = jnp.where(lax.broadcasted_iota(jnp.int32, (8, 128), 0) < 4, high, low)
    rows = jnp.concatenate([total[0:32], piece], axis=0).astype(BF16)
    o_ref[...] = jnp.broadcast_to(rows[None], (N, 40, 128))
    right_ref[...] = total[32:40]
    first = lax.axis_index("zh") == 0
    eig_ref[0:8] = jnp.where(first, a_ref[48:56], b_ref[48:56])
    eig_ref[8:16] = jnp.where(first, b_ref[48:56], a_ref[48:56])


def rotate(r_ref, g_ref, bo_ref, right_ref, o_ref, w_ref):
    proj = r_ref[:, 0:32, :].reshape(N * 32, 128)
    moment = jnp.dot(g_ref[...], proj, preferred_element_type=F32)
    m1, rest = split(moment)
    m2, m3 = split(rest)
    rotated = tn(bo_ref[...], jnp.concatenate([m1, m2, m3], axis=1).astype(BF16))
    rotated = (rotated[:, 256:384] + rotated[:, 128:256]) + rotated[:, 0:128]
    o_ref[:, 0:8, :] = rotated[0:256].reshape(N, 8, 128)
    o_ref[:, 8:16, :] = rotated[256:512].reshape(N, 8, 128)
    pieces = r_ref[:, 32:40, :].astype(F32)
    pieces = (pieces + jnp.roll(pieces, 4, axis=1)).reshape(N // 2, 2, 8, 128)
    top = lax.broadcasted_iota(jnp.int32, (N // 2, 8, 128), 1) < 4
    left = jnp.where(top, pieces[:, 0], pieces[:, 1]).reshape(128, 128)
    right = right_ref[...]
    rows = jnp.concatenate([right, right, right, right], axis=0)
    query = lax.broadcasted_iota(jnp.int32, (32, 128), 0) // 8
    column = lax.broadcasted_iota(jnp.int32, (32, 128), 1) // 32
    rows = jnp.where(query == column, rows, 0.0)
    w_ref[...] = jnp.dot(rows, left, precision=lax.Precision.HIGHEST, preferred_element_type=F32)


def column_pack(r_ref, w_ref, o_ref, s_ref):
    total = jnp.sum(r_ref[...], axis=0)
    zh = lax.axis_index("zh")
    mine = w_ref[pl.ds(pl.multiple_of(zh * 16, 16), 16)]
    o_ref[...] = jnp.broadcast_to(mine[None], (16, 16, 128))
    o_ref[2 * lax.axis_index("dp") + 1 - zh] = total
    s_ref[...] = total


def score(r_ref, s_ref, w_ref, eig_ref, d_ref, o_ref):
    zh = lax.axis_index("zh")
    partner = 2 * lax.axis_index("dp") + 1 - zh
    damped = (s_ref[...] + r_ref[partner]) / (eig_ref[...] + damping)
    d_ref[...] = jnp.where(zh == 0, damped[0:8], damped[8:16])
    local = w_ref[pl.ds(pl.multiple_of((1 - zh) * 16, 16), 16)]

    def weights(source, rows):
        return jnp.where(partner == source, local[rows], r_ref[source, rows])

    sums = []
    for q in range(16):
        rows = slice((q % 2) * 8, (q % 2) * 8 + 8)
        even = 4 * (q // 4) + (q % 4) // 2
        part = weights(even, rows) * damped[0:8] + weights(even + 2, rows) * damped[8:16]
        sums.append(jnp.sum(part, axis=0, keepdims=True))
    sums = jnp.concatenate(sums, axis=0)
    ones = jnp.ones((8, 128), F32)
    row = lax.dot_general(ones, jnp.concatenate([sums, jnp.zeros((112, 128), F32)], axis=0),
                          (((1,), (1,)), ((), ())), precision=lax.Precision.HIGHEST, preferred_element_type=F32)
    o_ref[...] = jnp.broadcast_to(row[None, 0:1], (N, 1, 128))


def last_sum(r_ref, o_ref):
    o_ref[...] = jnp.sum(r_ref[...], axis=0)[:, 0:16]


def on_device(train_inputs, out_grads, basis_in, basis_out, query_left, query_right, eigenvalues):
    def shape(*dims, dtype=F32):
        return jax.ShapeDtypeStruct(dims, dtype)

    hbm = pl.BlockSpec(memory_space=pltpu.HBM)
    part = pl.pallas_call(
        partials,
        out_shape=shape(N, 88, 128, dtype=BF16),
        in_specs=[hbm] * 5,
        scratch_shapes=[
            pltpu.VMEM((1024, 128), BF16),
            pltpu.VMEM((128, 128), BF16),
            pltpu.VMEM((128, 128), BF16),
            pltpu.VMEM((448, 256), BF16),
            pltpu.VMEM((448, 128), BF16),
            pltpu.SemaphoreType.DMA((5,)),
        ],
        compiler_params=pltpu.CompilerParams(vmem_limit_bytes=12 * 1024 * 1024),
    )(*(pltpu.with_memory_space_constraint(v, pltpu.HBM) for v in (train_inputs, basis_in, query_left, basis_out, query_right)))
    part = lax.all_to_all(part, PLANE, 0, 0, tiled=True)
    mine = call(plane_sum, shape(56, 128), part, eigenvalues.T)
    other = lax.ppermute(mine, "zh", [(0, 1), (1, 0)])
    full, right, eig = call(
        finish, (shape(N, 40, 128, dtype=BF16), shape(8, 128), shape(16, 128)), mine, other)
    full = lax.all_to_all(full, PLANE, 0, 0, tiled=True)
    rotated, weights = call(
        rotate, (shape(N, 16, 128), shape(32, 128)), full, out_grads.T, basis_out, right)
    rotated = lax.all_to_all(rotated, PLANE, 0, 0, tiled=True)
    packed, half = call(column_pack, (shape(16, 16, 128), shape(16, 128)), rotated, weights)
    packed = lax.all_to_all(packed, COLUMN, 0, 0, tiled=True)
    damped, scores = call(score, (shape(8, 128), shape(N, 1, 128)), packed, half, weights, eig)
    scores = lax.all_to_all(scores, PLANE, 0, 0, tiled=True)
    scores = call(last_sum, shape(1, 16), scores)
    return scores, damped.T[None]


def solution(mesh):
    fine = Mesh(mesh.devices.reshape(8, 2, 8, 4), ("dp", "zh", "y", "x"))
    basis = ("zh", "y", "x")
    in_specs = (
        P("dp", basis),
        P("dp", basis),
        P(basis, None),
        P(basis, None),
        P(basis, None),
        P(basis, None),
        P(None, basis),
    )
    out_specs = (P("dp", None), P("dp", None, basis))
    return jax.shard_map(
        on_device, mesh=fine, in_specs=in_specs, out_specs=out_specs, check_vma=False
    )
```

```python
import jax
import jax.numpy as jnp
from jax import lax
from jax.experimental import pallas as pl
from jax.experimental.pallas import tpu as pltpu
from jax.sharding import Mesh, PartitionSpec as P

F32 = jnp.float32
BF16 = jnp.bfloat16
damping = 0.1

PLANE = ("y", "x")
COLUMN = ("dp", "zh")
N = 32


def tn(a, b):
    return lax.dot_general(a, b, (((0,), (0,)), ((), ())), preferred_element_type=F32)


def call(kernel, out_shape, *args):
    return pl.pallas_call(
        kernel,
        out_shape=out_shape,
        compiler_params=pltpu.CompilerParams(vmem_limit_bytes=12 * 1024 * 1024),
    )(*args)


def split(value):
    high = value.astype(BF16).astype(F32)
    return high, value - high


def partials(x_hbm, bi_hbm, ql_hbm, bo_hbm, qr_hbm, o_ref, x_ref, bi_ref, ql_ref, bo_ref, qr_ref, sem):
    dp = lax.axis_index("dp")
    block = pl.ds(pl.multiple_of((dp // 2) * 128, 128), 128)
    half = pl.ds(pl.multiple_of((dp % 2) * 256, 128), 256)
    moves = [
        (bi_hbm, bi_ref), (x_hbm, x_ref), (ql_hbm.at[:, block], ql_ref),
        (qr_hbm.at[:, block], qr_ref), (bo_hbm.at[:, half], bo_ref),
    ]
    moves = [pltpu.make_async_copy(src, dst, sem.at[k]) for k, (src, dst) in enumerate(moves)]
    for move in moves:
        move.start()
    moves[0].wait()
    moves[1].wait()
    proj = jnp.dot(x_ref[...], bi_ref[...], preferred_element_type=F32)
    high, low = split(proj)
    o_ref[:, 0:32, :] = high.astype(BF16).reshape(N, 32, 128)
    o_ref[:, 32:64, :] = low.astype(BF16).reshape(N, 32, 128)
    moves[2].wait()
    high, low = split(tn(ql_ref[...], bi_ref[...]).reshape(N // 2, 8, 128))
    top = lax.broadcasted_iota(jnp.int32, (N // 2, 8, 128), 1) < 4
    even = jnp.where(top, high, jnp.roll(low, 4, axis=1))
    odd = jnp.where(top, jnp.roll(high, 4, axis=1), low)
    left = jnp.concatenate([even[:, None], odd[:, None]], axis=1).reshape(N, 8, 128)
    moves[3].wait()
    moves[4].wait()
    high, low = split(tn(bo_ref[...], qr_ref[...]).reshape(N, 8, 128))
    o_ref[:, 64:88, :] = jnp.concatenate([high, low, left], axis=1).astype(BF16)


def plane_sum(r_ref, eig_ref, o_ref):
    total = jnp.sum(r_ref[...].astype(F32), axis=0)
    o_ref[0:32] = total[0:32] + total[32:64]
    o_ref[32:40] = total[64:72] + total[72:80]
    o_ref[40:48] = total[80:88]
    o_ref[48:56] = eig_ref[...]


def finish(a_ref, b_ref, o_ref, right_ref, eig_ref):
    total = a_ref[0:48] + b_ref[0:48]
    left = total[40:48] + jnp.roll(total[40:48], 4, axis=0)
    high, low = split(left)
    piece = jnp.where(lax.broadcasted_iota(jnp.int32, (8, 128), 0) < 4, high, low)
    rows = jnp.concatenate([total[0:32], piece], axis=0).astype(BF16)
    o_ref[...] = jnp.broadcast_to(rows[None], (N, 40, 128))
    right_ref[...] = total[32:40]
    first = lax.axis_index("zh") == 0
    eig_ref[0:8] = jnp.where(first, a_ref[48:56], b_ref[48:56])
    eig_ref[8:16] = jnp.where(first, b_ref[48:56], a_ref[48:56])


def rotate(r_ref, g_ref, bo_ref, right_ref, o_ref, w_ref):
    proj = r_ref[:, 0:32, :].reshape(N * 32, 128)
    moment = jnp.dot(g_ref[...], proj, preferred_element_type=F32)
    m1, rest = split(moment)
    m2, m3 = split(rest)
    rotated = tn(bo_ref[...], jnp.concatenate([m1, m2, m3], axis=1).astype(BF16))
    rotated = (rotated[:, 256:384] + rotated[:, 128:256]) + rotated[:, 0:128]
    o_ref[:, 0:8, :] = rotated[0:256].reshape(N, 8, 128)
    o_ref[:, 8:16, :] = rotated[256:512].reshape(N, 8, 128)
    pieces = r_ref[:, 32:40, :].astype(F32)
    pieces = (pieces + jnp.roll(pieces, 4, axis=1)).reshape(N // 2, 2, 8, 128)
    top = lax.broadcasted_iota(jnp.int32, (N // 2, 8, 128), 1) < 4
    left = jnp.where(top, pieces[:, 0], pieces[:, 1]).reshape(128, 128)
    right = right_ref[...]
    rows = jnp.concatenate([right, right, right, right], axis=0)
    query = lax.broadcasted_iota(jnp.int32, (32, 128), 0) // 8
    column = lax.broadcasted_iota(jnp.int32, (32, 128), 1) // 32
    rows = jnp.where(query == column, rows, 0.0)
    w_ref[...] = jnp.dot(rows, left, precision=lax.Precision.HIGHEST, preferred_element_type=F32)


def column_pack(r_ref, w_ref, o_ref, s_ref):
    total = jnp.sum(r_ref[...], axis=0)
    zh = lax.axis_index("zh")
    mine = w_ref[pl.ds(pl.multiple_of(zh * 16, 16), 16)]
    o_ref[...] = jnp.broadcast_to(mine[None], (16, 16, 128))
    o_ref[2 * lax.axis_index("dp") + 1 - zh] = total
    s_ref[...] = total


def score(r_ref, s_ref, w_ref, eig_ref, d_ref, o_ref):
    zh = lax.axis_index("zh")
    partner = 2 * lax.axis_index("dp") + 1 - zh
    damped = (s_ref[...] + r_ref[partner]) / (eig_ref[...] + damping)
    d_ref[...] = jnp.where(zh == 0, damped[0:8], damped[8:16])
    local = w_ref[pl.ds(pl.multiple_of((1 - zh) * 16, 16), 16)]

    def weights(source, rows):
        return jnp.where(partner == source, local[rows], r_ref[source, rows])

    sums = []
    for q in range(16):
        rows = slice((q % 2) * 8, (q % 2) * 8 + 8)
        even = 4 * (q // 4) + (q % 4) // 2
        part = weights(even, rows) * damped[0:8] + weights(even + 2, rows) * damped[8:16]
        sums.append(jnp.sum(part, axis=0, keepdims=True))
    sums = jnp.concatenate(sums, axis=0)
    ones = jnp.ones((8, 128), F32)
    row = lax.dot_general(ones, jnp.concatenate([sums, jnp.zeros((112, 128), F32)], axis=0),
                          (((1,), (1,)), ((), ())), precision=lax.Precision.HIGHEST, preferred_element_type=F32)
    o_ref[...] = jnp.broadcast_to(row[None, 0:1], (N, 1, 128))


def last_sum(r_ref, d_ref, o_ref, e_ref):
    o_ref[...] = jnp.sum(r_ref[...], axis=0)[:, 0:16]
    e_ref[...] = d_ref[...]


def on_device(train_inputs, out_grads, basis_in, basis_out, query_left, query_right, eigenvalues):
    def shape(*dims, dtype=F32):
        return jax.ShapeDtypeStruct(dims, dtype)

    hbm = pl.BlockSpec(memory_space=pltpu.HBM)
    part = pl.pallas_call(
        partials,
        out_shape=shape(N, 88, 128, dtype=BF16),
        in_specs=[hbm] * 5,
        scratch_shapes=[
            pltpu.VMEM((1024, 128), BF16),
            pltpu.VMEM((128, 128), BF16),
            pltpu.VMEM((128, 128), BF16),
            pltpu.VMEM((448, 256), BF16),
            pltpu.VMEM((448, 128), BF16),
            pltpu.SemaphoreType.DMA((5,)),
        ],
        compiler_params=pltpu.CompilerParams(vmem_limit_bytes=12 * 1024 * 1024),
    )(*(pltpu.with_memory_space_constraint(v, pltpu.HBM) for v in (train_inputs, basis_in, query_left, basis_out, query_right)))
    part = lax.all_to_all(part, PLANE, 0, 0, tiled=True)
    mine = call(plane_sum, shape(56, 128), part, eigenvalues.T)
    other = lax.ppermute(mine, "zh", [(0, 1), (1, 0)])
    full, right, eig = call(
        finish, (shape(N, 40, 128, dtype=BF16), shape(8, 128), shape(16, 128)), mine, other)
    full = lax.all_to_all(full, PLANE, 0, 0, tiled=True)
    rotated, weights = call(
        rotate, (shape(N, 16, 128), shape(32, 128)), full, out_grads.T, basis_out, right)
    rotated = lax.all_to_all(rotated, PLANE, 0, 0, tiled=True)
    packed, half = call(column_pack, (shape(16, 16, 128), shape(16, 128)), rotated, weights)
    packed = lax.all_to_all(packed, COLUMN, 0, 0, tiled=True)
    damped, scores = call(score, (shape(8, 128), shape(N, 1, 128)), packed, half, weights, eig)
    scores = lax.all_to_all(scores, PLANE, 0, 0, tiled=True)
    scores, damped = call(last_sum, (shape(1, 16), shape(8, 128)), scores, damped)
    return scores, damped.T[None]


def solution(mesh):
    fine = Mesh(mesh.devices.reshape(8, 2, 8, 4), ("dp", "zh", "y", "x"))
    basis = ("zh", "y", "x")
    in_specs = (
        P("dp", basis),
        P("dp", basis),
        P(basis, None),
        P(basis, None),
        P(basis, None),
        P(basis, None),
        P(None, basis),
    )
    out_specs = (P("dp", None), P("dp", None, basis))
    return jax.shard_map(
        on_device, mesh=fine, in_specs=in_specs, out_specs=out_specs, check_vma=False
    )
```

```python
import jax
import jax.numpy as jnp
from jax import lax
from jax.experimental import pallas as pl
from jax.experimental.pallas import tpu as pltpu
from jax.sharding import Mesh, PartitionSpec as P

F32 = jnp.float32
BF16 = jnp.bfloat16
damping = 0.1

PLANE = ("y", "x")
COLUMN = ("dp", "zh")
N = 32
LOW = 16
TAIL = 32 + LOW


def tn(a, b):
    return lax.dot_general(a, b, (((0,), (0,)), ((), ())), preferred_element_type=F32)


def call(kernel, out_shape, *args):
    return pl.pallas_call(
        kernel,
        out_shape=out_shape,
        compiler_params=pltpu.CompilerParams(vmem_limit_bytes=12 * 1024 * 1024),
    )(*args)


def split(value):
    high = value.astype(BF16).astype(F32)
    return high, value - high


def partials(x_hbm, bi_hbm, ql_hbm, bo_hbm, qr_hbm, o_ref, x_ref, bi_ref, ql_ref, bo_ref, qr_ref, sem):
    dp = lax.axis_index("dp")
    block = pl.ds(pl.multiple_of((dp // 2) * 128, 128), 128)
    half = pl.ds(pl.multiple_of((dp % 2) * 256, 128), 256)
    moves = [
        (bi_hbm, bi_ref), (x_hbm, x_ref), (ql_hbm.at[:, block], ql_ref),
        (qr_hbm.at[:, block], qr_ref), (bo_hbm.at[:, half], bo_ref),
    ]
    moves = [
        pltpu.make_async_copy(src, dst, sem.at[k]) for k, (src, dst) in enumerate(moves)
    ]
    for move in moves:
        move.start()
    moves[0].wait()
    moves[1].wait()
    proj = jnp.dot(x_ref[...], bi_ref[...], preferred_element_type=F32)
    high, low = split(proj)
    o_ref[:, 0:32, :] = high.astype(BF16).reshape(N, 32, 128)
    o_ref[:, 32:TAIL, :] = low.astype(BF16).reshape(N, 32, 128)[:, 0:LOW]
    moves[2].wait()
    high, low = split(tn(ql_ref[...], bi_ref[...]).reshape(N // 2, 8, 128))
    top = lax.broadcasted_iota(jnp.int32, (N // 2, 8, 128), 1) < 4
    even = jnp.where(top, high, jnp.roll(low, 4, axis=1))
    odd = jnp.where(top, jnp.roll(high, 4, axis=1), low)
    left = jnp.concatenate([even[:, None], odd[:, None]], axis=1).reshape(N, 8, 128)
    moves[3].wait()
    moves[4].wait()
    high, low = split(tn(bo_ref[...], qr_ref[...]).reshape(N, 8, 128))
    o_ref[:, TAIL : TAIL + 24, :] = jnp.concatenate([high, low, left], axis=1).astype(BF16)


def plane_sum(r_ref, eig_ref, o_ref):
    total = jnp.sum(r_ref[...].astype(F32), axis=0)
    rest = total[TAIL:]
    o_ref[0:LOW] = total[0:LOW] + total[32:TAIL]
    o_ref[LOW:32] = total[LOW:32]
    o_ref[32:40] = rest[0:8] + rest[8:16]
    o_ref[40:48] = rest[16:24]
    o_ref[48:56] = eig_ref[...]


def finish(a_ref, b_ref, o_ref, right_ref, eig_ref):
    total = a_ref[0:48] + b_ref[0:48]
    left = total[40:48] + jnp.roll(total[40:48], 4, axis=0)
    high, low = split(left)
    piece = jnp.where(lax.broadcasted_iota(jnp.int32, (8, 128), 0) < 4, high, low)
    rows = jnp.concatenate([total[0:32], piece], axis=0).astype(BF16)
    o_ref[...] = jnp.broadcast_to(rows[None], (N, 40, 128))
    right_ref[...] = total[32:40]
    first = lax.axis_index("zh") == 0
    eig_ref[0:8] = jnp.where(first, a_ref[48:56], b_ref[48:56])
    eig_ref[8:16] = jnp.where(first, b_ref[48:56], a_ref[48:56])


def rotate(r_ref, g_ref, bo_ref, right_ref, o_ref, w_ref):
    proj = r_ref[:, 0:32, :].reshape(N * 32, 128)
    moment = jnp.dot(g_ref[...], proj, preferred_element_type=F32)
    m1, rest = split(moment)
    m2, m3 = split(rest)
    rotated = tn(bo_ref[...], jnp.concatenate([m1, m2, m3], axis=1).astype(BF16))
    rotated = (rotated[:, 256:384] + rotated[:, 128:256]) + rotated[:, 0:128]
    o_ref[:, 0:8, :] = rotated[0:256].reshape(N, 8, 128)
    o_ref[:, 8:16, :] = rotated[256:512].reshape(N, 8, 128)
    pieces = r_ref[:, 32:40, :].astype(F32)
    pieces = (pieces + jnp.roll(pieces, 4, axis=1)).reshape(N // 2, 2, 8, 128)
    top = lax.broadcasted_iota(jnp.int32, (N // 2, 8, 128), 1) < 4
    left = jnp.where(top, pieces[:, 0], pieces[:, 1]).reshape(128, 128)
    right = right_ref[...]
    rows = jnp.concatenate([right, right, right, right], axis=0)
    query = lax.broadcasted_iota(jnp.int32, (32, 128), 0) // 8
    column = lax.broadcasted_iota(jnp.int32, (32, 128), 1) // 32
    rows = jnp.where(query == column, rows, 0.0)
    w_ref[...] = jnp.dot(rows, left, precision=lax.Precision.HIGHEST, preferred_element_type=F32)


def column_pack(r_ref, w_ref, o_ref, s_ref):
    total = jnp.sum(r_ref[...], axis=0)
    zh = lax.axis_index("zh")
    mine = w_ref[pl.ds(pl.multiple_of(zh * 16, 16), 16)]
    o_ref[...] = jnp.broadcast_to(mine[None], (16, 16, 128))
    o_ref[2 * lax.axis_index("dp") + 1 - zh] = total
    s_ref[...] = total


def score(r_ref, s_ref, w_ref, eig_ref, d_ref, o_ref):
    zh = lax.axis_index("zh")
    partner = 2 * lax.axis_index("dp") + 1 - zh
    damped = (s_ref[...] + r_ref[partner]) / (eig_ref[...] + damping)
    d_ref[...] = jnp.where(zh == 0, damped[0:8], damped[8:16])
    local = w_ref[pl.ds(pl.multiple_of((1 - zh) * 16, 16), 16)]

    def weights(source, rows):
        return jnp.where(partner == source, local[rows], r_ref[source, rows])

    sums = []
    for q in range(16):
        rows = slice((q % 2) * 8, (q % 2) * 8 + 8)
        even = 4 * (q // 4) + (q % 4) // 2
        part = weights(even, rows) * damped[0:8] + weights(even + 2, rows) * damped[8:16]
        sums.append(jnp.sum(part, axis=0, keepdims=True))
    sums = jnp.concatenate(sums, axis=0)
    ones = jnp.ones((8, 128), F32)
    row = lax.dot_general(ones, jnp.concatenate([sums, jnp.zeros((112, 128), F32)], axis=0),
                          (((1,), (1,)), ((), ())), precision=lax.Precision.HIGHEST, preferred_element_type=F32)
    o_ref[...] = jnp.broadcast_to(row[None, 0:1], (N, 1, 128))


def last_sum(r_ref, d_ref, o_ref, e_ref):
    o_ref[...] = jnp.sum(r_ref[...], axis=0)[:, 0:16]
    e_ref[...] = d_ref[...]


def on_device(train_inputs, out_grads, basis_in, basis_out, query_left, query_right, eigenvalues):
    def shape(*dims, dtype=F32):
        return jax.ShapeDtypeStruct(dims, dtype)

    hbm = pl.BlockSpec(memory_space=pltpu.HBM)
    part = pl.pallas_call(
        partials,
        out_shape=shape(N, TAIL + 24, 128, dtype=BF16),
        in_specs=[hbm] * 5,
        scratch_shapes=[
            pltpu.VMEM((1024, 128), BF16),
            pltpu.VMEM((128, 128), BF16),
            pltpu.VMEM((128, 128), BF16),
            pltpu.VMEM((448, 256), BF16),
            pltpu.VMEM((448, 128), BF16),
            pltpu.SemaphoreType.DMA((5,)),
        ],
        compiler_params=pltpu.CompilerParams(vmem_limit_bytes=12 * 1024 * 1024),
    )(*(pltpu.with_memory_space_constraint(v, pltpu.HBM) for v in (train_inputs, basis_in, query_left, basis_out, query_right)))
    part = lax.all_to_all(part, PLANE, 0, 0, tiled=True)
    mine = call(plane_sum, shape(56, 128), part, eigenvalues.T)
    other = lax.ppermute(mine, "zh", [(0, 1), (1, 0)])
    full, right, eig = call(
        finish, (shape(N, 40, 128, dtype=BF16), shape(8, 128), shape(16, 128)), mine, other)
    full = lax.all_to_all(full, PLANE, 0, 0, tiled=True)
    rotated, weights = call(
        rotate, (shape(N, 16, 128), shape(32, 128)), full, out_grads.T, basis_out, right)
    rotated = lax.all_to_all(rotated, PLANE, 0, 0, tiled=True)
    packed, half = call(column_pack, (shape(16, 16, 128), shape(16, 128)), rotated, weights)
    packed = lax.all_to_all(packed, COLUMN, 0, 0, tiled=True)
    damped, scores = call(score, (shape(8, 128), shape(N, 1, 128)), packed, half, weights, eig)
    scores = lax.all_to_all(scores, PLANE, 0, 0, tiled=True)
    scores, damped = call(last_sum, (shape(1, 16), shape(8, 128)), scores, damped)
    return scores, damped.T[None]


def solution(mesh):
    fine = Mesh(mesh.devices.reshape(8, 2, 8, 4), ("dp", "zh", "y", "x"))
    basis = ("zh", "y", "x")
    in_specs = (
        P("dp", basis),
        P("dp", basis),
        P(basis, None),
        P(basis, None),
        P(basis, None),
        P(basis, None),
        P(None, basis),
    )
    out_specs = (P("dp", None), P("dp", None, basis))
    return jax.shard_map(
        on_device, mesh=fine, in_specs=in_specs, out_specs=out_specs, check_vma=False
    )
```

```python
import jax
import jax.numpy as jnp
from jax import lax
from jax.experimental import pallas as pl
from jax.experimental.pallas import tpu as pltpu
from jax.sharding import Mesh, PartitionSpec as P

F32 = jnp.float32
BF16 = jnp.bfloat16
damping = 0.1

PLANE = ("y", "x")
COLUMN = ("dp", "zh")
N = 32
LOW = 16
TAIL = 32 + LOW


def tn(a, b):
    return lax.dot_general(a, b, (((0,), (0,)), ((), ())), preferred_element_type=F32)


def call(kernel, out_shape, *args):
    return pl.pallas_call(
        kernel,
        out_shape=out_shape,
        compiler_params=pltpu.CompilerParams(vmem_limit_bytes=12 * 1024 * 1024),
    )(*args)


def split(value):
    high = value.astype(BF16).astype(F32)
    return high, value - high


def partials(x_hbm, bi_hbm, ql_hbm, bo_hbm, qr_hbm, o_ref, x_ref, bi_ref, ql_ref, bo_ref, qr_ref, sem):
    dp = lax.axis_index("dp")
    block = pl.ds(pl.multiple_of((dp // 2) * 128, 128), 128)
    half = pl.ds(pl.multiple_of((dp % 2) * 256, 128), 256)
    moves = [
        (bi_hbm, bi_ref), (x_hbm, x_ref), (ql_hbm.at[:, block], ql_ref),
        (qr_hbm.at[:, block], qr_ref), (bo_hbm.at[:, half], bo_ref),
    ]
    moves = [
        pltpu.make_async_copy(src, dst, sem.at[k]) for k, (src, dst) in enumerate(moves)
    ]
    for move in moves:
        move.start()
    moves[0].wait()
    moves[1].wait()
    proj = jnp.dot(x_ref[...], bi_ref[...], preferred_element_type=F32)
    high, low = split(proj)
    o_ref[:, 0:32, :] = high.astype(BF16).reshape(N, 32, 128)
    o_ref[:, 32:TAIL, :] = low.astype(BF16).reshape(N, 32, 128)[:, 0:LOW]
    moves[2].wait()
    high, low = split(tn(ql_ref[...], bi_ref[...]).reshape(N // 2, 8, 128))
    top = lax.broadcasted_iota(jnp.int32, (N // 2, 8, 128), 1) < 4
    even = jnp.where(top, high, jnp.roll(low, 4, axis=1))
    odd = jnp.where(top, jnp.roll(high, 4, axis=1), low)
    left = jnp.concatenate([even[:, None], odd[:, None]], axis=1).reshape(N, 8, 128)
    moves[3].wait()
    moves[4].wait()
    high, low = split(tn(bo_ref[...], qr_ref[...]).reshape(N, 8, 128))
    o_ref[:, TAIL : TAIL + 24, :] = jnp.concatenate([high, low, left], axis=1).astype(BF16)


def plane_sum(r_ref, eig_ref, o_ref):
    total = jnp.sum(r_ref[...].astype(F32), axis=0)
    rest = total[TAIL:]
    o_ref[0:LOW] = total[0:LOW] + total[32:TAIL]
    o_ref[LOW:32] = total[LOW:32]
    o_ref[32:40] = rest[0:8] + rest[8:16]
    o_ref[40:48] = rest[16:24]
    o_ref[48:56] = eig_ref[...]


def finish(a_ref, b_ref, o_ref, right_ref, eig_ref):
    total = a_ref[0:48] + b_ref[0:48]
    left = total[40:48] + jnp.roll(total[40:48], 4, axis=0)
    high, low = split(left)
    piece = jnp.where(lax.broadcasted_iota(jnp.int32, (8, 128), 0) < 4, high, low)
    rows = jnp.concatenate([total[0:32], piece], axis=0).astype(BF16)
    o_ref[...] = jnp.broadcast_to(rows[None], (N, 40, 128))
    right_ref[...] = total[32:40]
    first = lax.axis_index("zh") == 0
    eig_ref[0:8] = jnp.where(first, a_ref[48:56], b_ref[48:56])
    eig_ref[8:16] = jnp.where(first, b_ref[48:56], a_ref[48:56])


def rotate(r_ref, g_ref, bo_ref, right_ref, o_ref, w_ref):
    proj = r_ref[:, 0:32, :].reshape(N * 32, 128)
    moment = jnp.dot(g_ref[...], proj, preferred_element_type=F32)
    rotated = tn(bo_ref[...], jnp.concatenate(split(moment), axis=1).astype(BF16))
    rotated = rotated[:, 128:256] + rotated[:, 0:128]
    o_ref[:, 0:8, :] = rotated[0:256].reshape(N, 8, 128)
    o_ref[:, 8:16, :] = rotated[256:512].reshape(N, 8, 128)
    pieces = r_ref[:, 32:40, :].astype(F32)
    pieces = (pieces + jnp.roll(pieces, 4, axis=1)).reshape(N // 2, 2, 8, 128)
    top = lax.broadcasted_iota(jnp.int32, (N // 2, 8, 128), 1) < 4
    left = jnp.where(top, pieces[:, 0], pieces[:, 1]).reshape(128, 128)
    right = right_ref[...]
    rows = jnp.concatenate([right, right, right, right], axis=0)
    query = lax.broadcasted_iota(jnp.int32, (32, 128), 0) // 8
    column = lax.broadcasted_iota(jnp.int32, (32, 128), 1) // 32
    rows = jnp.where(query == column, rows, 0.0)
    w_ref[...] = jnp.dot(rows, left, precision=lax.Precision.HIGHEST, preferred_element_type=F32)


def column_pack(r_ref, w_ref, o_ref, s_ref):
    total = jnp.sum(r_ref[...], axis=0)
    zh = lax.axis_index("zh")
    mine = w_ref[pl.ds(pl.multiple_of(zh * 16, 16), 16)]
    o_ref[...] = jnp.broadcast_to(mine[None], (16, 16, 128))
    o_ref[2 * lax.axis_index("dp") + 1 - zh] = total
    s_ref[...] = total


def score(r_ref, s_ref, w_ref, eig_ref, d_ref, o_ref):
    zh = lax.axis_index("zh")
    partner = 2 * lax.axis_index("dp") + 1 - zh
    damped = (s_ref[...] + r_ref[partner]) / (eig_ref[...] + damping)
    d_ref[...] = jnp.where(zh == 0, damped[0:8], damped[8:16])
    local = w_ref[pl.ds(pl.multiple_of((1 - zh) * 16, 16), 16)]

    def weights(source, rows):
        return jnp.where(partner == source, local[rows], r_ref[source, rows])

    sums = []
    for q in range(16):
        rows = slice((q % 2) * 8, (q % 2) * 8 + 8)
        even = 4 * (q // 4) + (q % 4) // 2
        part = weights(even, rows) * damped[0:8] + weights(even + 2, rows) * damped[8:16]
        sums.append(jnp.sum(part, axis=0, keepdims=True))
    sums = jnp.concatenate(sums, axis=0)
    ones = jnp.ones((8, 128), F32)
    row = lax.dot_general(ones, jnp.concatenate([sums, jnp.zeros((112, 128), F32)], axis=0),
                          (((1,), (1,)), ((), ())), precision=lax.Precision.HIGHEST, preferred_element_type=F32)
    o_ref[...] = jnp.broadcast_to(row[None, 0:1], (N, 1, 128))


def last_sum(r_ref, d_ref, o_ref, e_ref):
    o_ref[...] = jnp.sum(r_ref[...], axis=0)[:, 0:16]
    e_ref[...] = d_ref[...]


def on_device(train_inputs, out_grads, basis_in, basis_out, query_left, query_right, eigenvalues):
    def shape(*dims, dtype=F32):
        return jax.ShapeDtypeStruct(dims, dtype)

    hbm = pl.BlockSpec(memory_space=pltpu.HBM)
    part = pl.pallas_call(
        partials,
        out_shape=shape(N, TAIL + 24, 128, dtype=BF16),
        in_specs=[hbm] * 5,
        scratch_shapes=[
            pltpu.VMEM((1024, 128), BF16),
            pltpu.VMEM((128, 128), BF16),
            pltpu.VMEM((128, 128), BF16),
            pltpu.VMEM((448, 256), BF16),
            pltpu.VMEM((448, 128), BF16),
            pltpu.SemaphoreType.DMA((5,)),
        ],
        compiler_params=pltpu.CompilerParams(vmem_limit_bytes=12 * 1024 * 1024),
    )(*(pltpu.with_memory_space_constraint(v, pltpu.HBM) for v in (train_inputs, basis_in, query_left, basis_out, query_right)))
    part = lax.all_to_all(part, PLANE, 0, 0, tiled=True)
    mine = call(plane_sum, shape(56, 128), part, eigenvalues.T)
    other = lax.ppermute(mine, "zh", [(0, 1), (1, 0)])
    full, right, eig = call(
        finish, (shape(N, 40, 128, dtype=BF16), shape(8, 128), shape(16, 128)), mine, other)
    full = lax.all_to_all(full, PLANE, 0, 0, tiled=True)
    rotated, weights = call(
        rotate, (shape(N, 16, 128), shape(32, 128)), full, out_grads.T, basis_out, right)
    rotated = lax.all_to_all(rotated, PLANE, 0, 0, tiled=True)
    packed, half = call(column_pack, (shape(16, 16, 128), shape(16, 128)), rotated, weights)
    packed = lax.all_to_all(packed, COLUMN, 0, 0, tiled=True)
    damped, scores = call(score, (shape(8, 128), shape(N, 1, 128)), packed, half, weights, eig)
    scores = lax.all_to_all(scores, PLANE, 0, 0, tiled=True)
    scores, damped = call(last_sum, (shape(1, 16), shape(8, 128)), scores, damped)
    return scores, damped.T[None]


def solution(mesh):
    fine = Mesh(mesh.devices.reshape(8, 2, 8, 4), ("dp", "zh", "y", "x"))
    basis = ("zh", "y", "x")
    in_specs = (
        P("dp", basis),
        P("dp", basis),
        P(basis, None),
        P(basis, None),
        P(basis, None),
        P(basis, None),
        P(None, basis),
    )
    out_specs = (P("dp", None), P("dp", None, basis))
    return jax.shard_map(
        on_device, mesh=fine, in_specs=in_specs, out_specs=out_specs, check_vma=False
    )
```

```python
import jax
import jax.numpy as jnp
from jax import lax
from jax.experimental import pallas as pl
from jax.experimental.pallas import tpu as pltpu
from jax.sharding import Mesh, PartitionSpec as P

F32 = jnp.float32
BF16 = jnp.bfloat16
damping = 0.1

PLANE = ("y", "x")
COLUMN = ("dp", "zh")
N = 32
LOW = 16
TAIL = 32 + LOW


def tn(a, b):
    return lax.dot_general(a, b, (((0,), (0,)), ((), ())), preferred_element_type=F32)


def call(kernel, out_shape, *args):
    return pl.pallas_call(
        kernel,
        out_shape=out_shape,
        compiler_params=pltpu.CompilerParams(vmem_limit_bytes=12 * 1024 * 1024),
    )(*args)


def split(value):
    high = value.astype(BF16).astype(F32)
    return high, value - high


def partials(x_hbm, bi_hbm, ql_hbm, bo_hbm, qr_hbm, o_ref, x_ref, bi_ref, ql_ref, bo_ref, qr_ref, sem):
    dp = lax.axis_index("dp")
    block = pl.ds(pl.multiple_of((dp // 2) * 128, 128), 128)
    half = pl.ds(pl.multiple_of((dp % 2) * 256, 128), 256)
    moves = [
        (bi_hbm, bi_ref), (x_hbm, x_ref), (ql_hbm.at[:, block], ql_ref),
        (qr_hbm.at[:, block], qr_ref), (bo_hbm.at[:, half], bo_ref),
    ]
    moves = [
        pltpu.make_async_copy(src, dst, sem.at[k]) for k, (src, dst) in enumerate(moves)
    ]
    for move in moves:
        move.start()
    for move in moves:
        move.wait()
    proj = jnp.dot(x_ref[...], bi_ref[...], preferred_element_type=F32)
    high, low = split(proj)
    o_ref[:, 0:32, :] = high.astype(BF16).reshape(N, 32, 128)
    o_ref[:, 32:TAIL, :] = low.astype(BF16).reshape(N, 32, 128)[:, 0:LOW]
    high, low = split(tn(ql_ref[...], bi_ref[...]).reshape(N // 2, 8, 128))
    top = lax.broadcasted_iota(jnp.int32, (N // 2, 8, 128), 1) < 4
    even = jnp.where(top, high, jnp.roll(low, 4, axis=1))
    odd = jnp.where(top, jnp.roll(high, 4, axis=1), low)
    left = jnp.concatenate([even[:, None], odd[:, None]], axis=1).reshape(N, 8, 128)
    high, low = split(tn(bo_ref[...], qr_ref[...]).reshape(N, 8, 128))
    o_ref[:, TAIL : TAIL + 24, :] = jnp.concatenate([high, low, left], axis=1).astype(BF16)


def plane_sum(r_ref, eig_ref, o_ref):
    total = jnp.sum(r_ref[...].astype(F32), axis=0)
    rest = total[TAIL:]
    o_ref[0:LOW] = total[0:LOW] + total[32:TAIL]
    o_ref[LOW:32] = total[LOW:32]
    o_ref[32:40] = rest[0:8] + rest[8:16]
    o_ref[40:48] = rest[16:24]
    o_ref[48:56] = eig_ref[...]


def finish(a_ref, b_ref, o_ref, right_ref, eig_ref):
    total = a_ref[0:48] + b_ref[0:48]
    left = total[40:48] + jnp.roll(total[40:48], 4, axis=0)
    high, low = split(left)
    piece = jnp.where(lax.broadcasted_iota(jnp.int32, (8, 128), 0) < 4, high, low)
    rows = jnp.concatenate([total[0:32], piece], axis=0).astype(BF16)
    o_ref[...] = jnp.broadcast_to(rows[None], (N, 40, 128))
    right_ref[...] = total[32:40]
    first = lax.axis_index("zh") == 0
    eig_ref[0:8] = jnp.where(first, a_ref[48:56], b_ref[48:56])
    eig_ref[8:16] = jnp.where(first, b_ref[48:56], a_ref[48:56])


def rotate(r_ref, g_ref, bo_ref, right_ref, o_ref, w_ref):
    proj = r_ref[:, 0:32, :].reshape(N * 32, 128)
    moment = jnp.dot(g_ref[...], proj, preferred_element_type=F32)
    rotated = tn(bo_ref[...], jnp.concatenate(split(moment), axis=1).astype(BF16))
    rotated = rotated[:, 128:256] + rotated[:, 0:128]
    o_ref[:, 0:8, :] = rotated[0:256].reshape(N, 8, 128)
    o_ref[:, 8:16, :] = rotated[256:512].reshape(N, 8, 128)
    pieces = r_ref[:, 32:40, :].astype(F32)
    pieces = (pieces + jnp.roll(pieces, 4, axis=1)).reshape(N // 2, 2, 8, 128)
    top = lax.broadcasted_iota(jnp.int32, (N // 2, 8, 128), 1) < 4
    left = jnp.where(top, pieces[:, 0], pieces[:, 1]).reshape(128, 128)
    right = right_ref[...]
    rows = jnp.concatenate([right, right, right, right], axis=0)
    query = lax.broadcasted_iota(jnp.int32, (32, 128), 0) // 8
    column = lax.broadcasted_iota(jnp.int32, (32, 128), 1) // 32
    rows = jnp.where(query == column, rows, 0.0)
    w_ref[...] = jnp.dot(rows, left, precision=lax.Precision.HIGHEST, preferred_element_type=F32)


def column_pack(r_ref, w_ref, o_ref, s_ref):
    total = jnp.sum(r_ref[...], axis=0)
    zh = lax.axis_index("zh")
    mine = w_ref[pl.ds(pl.multiple_of(zh * 16, 16), 16)]
    o_ref[...] = jnp.broadcast_to(mine[None], (16, 16, 128))
    o_ref[2 * lax.axis_index("dp") + 1 - zh] = total
    s_ref[...] = total


def score(r_ref, s_ref, w_ref, eig_ref, d_ref, o_ref):
    zh = lax.axis_index("zh")
    partner = 2 * lax.axis_index("dp") + 1 - zh
    damped = (s_ref[...] + r_ref[partner]) / (eig_ref[...] + damping)
    d_ref[...] = jnp.where(zh == 0, damped[0:8], damped[8:16])
    local = w_ref[pl.ds(pl.multiple_of((1 - zh) * 16, 16), 16)]

    def weights(source, rows):
        return jnp.where(partner == source, local[rows], r_ref[source, rows])

    sums = []
    for q in range(16):
        rows = slice((q % 2) * 8, (q % 2) * 8 + 8)
        even = 4 * (q // 4) + (q % 4) // 2
        part = weights(even, rows) * damped[0:8] + weights(even + 2, rows) * damped[8:16]
        sums.append(jnp.sum(part, axis=0, keepdims=True))
    sums = jnp.concatenate(sums, axis=0)
    ones = jnp.ones((8, 128), F32)
    row = lax.dot_general(ones, jnp.concatenate([sums, jnp.zeros((112, 128), F32)], axis=0),
                          (((1,), (1,)), ((), ())), precision=lax.Precision.HIGHEST, preferred_element_type=F32)
    o_ref[...] = jnp.broadcast_to(row[None, 0:1], (N, 1, 128))


def last_sum(r_ref, d_ref, o_ref, e_ref):
    o_ref[...] = jnp.sum(r_ref[...], axis=0)[:, 0:16]
    e_ref[...] = d_ref[...]


def on_device(train_inputs, out_grads, basis_in, basis_out, query_left, query_right, eigenvalues):
    def shape(*dims, dtype=F32):
        return jax.ShapeDtypeStruct(dims, dtype)

    hbm = pl.BlockSpec(memory_space=pltpu.HBM)
    part = pl.pallas_call(
        partials,
        out_shape=shape(N, TAIL + 24, 128, dtype=BF16),
        in_specs=[hbm] * 5,
        scratch_shapes=[
            pltpu.VMEM((1024, 128), BF16),
            pltpu.VMEM((128, 128), BF16),
            pltpu.VMEM((128, 128), BF16),
            pltpu.VMEM((448, 256), BF16),
            pltpu.VMEM((448, 128), BF16),
            pltpu.SemaphoreType.DMA((5,)),
        ],
        compiler_params=pltpu.CompilerParams(vmem_limit_bytes=12 * 1024 * 1024),
    )(*(pltpu.with_memory_space_constraint(v, pltpu.HBM) for v in (train_inputs, basis_in, query_left, basis_out, query_right)))
    part = lax.all_to_all(part, PLANE, 0, 0, tiled=True)
    mine = call(plane_sum, shape(56, 128), part, eigenvalues.T)
    other = lax.ppermute(mine, "zh", [(0, 1), (1, 0)])
    full, right, eig = call(
        finish, (shape(N, 40, 128, dtype=BF16), shape(8, 128), shape(16, 128)), mine, other)
    full = lax.all_to_all(full, PLANE, 0, 0, tiled=True)
    rotated, weights = call(
        rotate, (shape(N, 16, 128), shape(32, 128)), full, out_grads.T, basis_out, right)
    rotated = lax.all_to_all(rotated, PLANE, 0, 0, tiled=True)
    packed, half = call(column_pack, (shape(16, 16, 128), shape(16, 128)), rotated, weights)
    packed = lax.all_to_all(packed, COLUMN, 0, 0, tiled=True)
    damped, scores = call(score, (shape(8, 128), shape(N, 1, 128)), packed, half, weights, eig)
    scores = lax.all_to_all(scores, PLANE, 0, 0, tiled=True)
    scores, damped = call(last_sum, (shape(1, 16), shape(8, 128)), scores, damped)
    return scores, damped.T[None]


def solution(mesh):
    fine = Mesh(mesh.devices.reshape(8, 2, 8, 4), ("dp", "zh", "y", "x"))
    basis = ("zh", "y", "x")
    in_specs = (
        P("dp", basis),
        P("dp", basis),
        P(basis, None),
        P(basis, None),
        P(basis, None),
        P(basis, None),
        P(None, basis),
    )
    out_specs = (P("dp", None), P("dp", None, basis))
    return jax.shard_map(
        on_device, mesh=fine, in_specs=in_specs, out_specs=out_specs, check_vma=False
    )
```

```python
import jax
import jax.numpy as jnp
from jax import lax
from jax.experimental import pallas as pl
from jax.experimental.pallas import tpu as pltpu
from jax.sharding import Mesh, PartitionSpec as P

F32 = jnp.float32
BF16 = jnp.bfloat16
damping = 0.1

PLANE = ("y", "x")
COLUMN = ("dp", "zh")
N = 32
LOW = 16
TAIL = 32 + LOW


def tn(a, b):
    return lax.dot_general(a, b, (((0,), (0,)), ((), ())), preferred_element_type=F32)


def call(kernel, out_shape, *args):
    return pl.pallas_call(
        kernel,
        out_shape=out_shape,
        compiler_params=pltpu.CompilerParams(vmem_limit_bytes=12 * 1024 * 1024),
    )(*args)


def split(value):
    high = value.astype(BF16).astype(F32)
    return high, value - high


def partials(x_hbm, bi_hbm, ql_hbm, bo_hbm, qr_hbm, o_ref, x_ref, bi_ref, ql_ref, bo_ref, qr_ref, sem):
    dp = lax.axis_index("dp")
    block = pl.ds(pl.multiple_of((dp // 2) * 128, 128), 128)
    half = pl.ds(pl.multiple_of((dp % 2) * 256, 128), 256)
    moves = [
        (bi_hbm, bi_ref), (x_hbm, x_ref), (ql_hbm.at[:, block], ql_ref),
        (qr_hbm.at[:, block], qr_ref), (bo_hbm.at[:, half], bo_ref),
    ]
    moves = [
        pltpu.make_async_copy(src, dst, sem.at[k]) for k, (src, dst) in enumerate(moves)
    ]
    for move in moves:
        move.start()
    for move in moves:
        move.wait()
    proj = jnp.dot(x_ref[...], bi_ref[...], preferred_element_type=F32)
    high, low = split(proj)
    o_ref[:, 0:32, :] = high.astype(BF16).reshape(N, 32, 128)
    o_ref[:, 32:TAIL, :] = low.astype(BF16).reshape(N, 32, 128)[:, 0:LOW]
    high, low = split(tn(ql_ref[...], bi_ref[...]).reshape(N // 2, 8, 128))
    top = lax.broadcasted_iota(jnp.int32, (N // 2, 8, 128), 1) < 4
    even = jnp.where(top, high, jnp.roll(low, 4, axis=1))
    odd = jnp.where(top, jnp.roll(high, 4, axis=1), low)
    left = jnp.concatenate([even[:, None], odd[:, None]], axis=1).reshape(N, 8, 128)
    high, low = split(tn(bo_ref[...], qr_ref[...]).reshape(N, 8, 128))
    o_ref[:, TAIL : TAIL + 24, :] = jnp.concatenate([high, low, left], axis=1).astype(BF16)


def plane_sum(r_ref, eig_ref, o_ref):
    total = jnp.sum(r_ref[...].astype(F32), axis=0)
    rest = total[TAIL:]
    o_ref[0:LOW] = total[0:LOW] + total[32:TAIL]
    o_ref[LOW:32] = total[LOW:32]
    o_ref[32:40] = rest[0:8] + rest[8:16]
    o_ref[40:48] = rest[16:24]
    o_ref[48:56] = eig_ref[...]


def finish(a_ref, b_ref, o_ref, right_ref, eig_ref):
    total = a_ref[0:48] + b_ref[0:48]
    left = total[40:48] + jnp.roll(total[40:48], 4, axis=0)
    high, low = split(left)
    piece = jnp.where(lax.broadcasted_iota(jnp.int32, (8, 128), 0) < 4, high, low)
    rows = jnp.concatenate([total[0:32], piece], axis=0).astype(BF16)
    o_ref[...] = jnp.broadcast_to(rows[None], (N, 40, 128))
    right_ref[...] = total[32:40]
    first = lax.axis_index("zh") == 0
    eig_ref[0:8] = jnp.where(first, a_ref[48:56], b_ref[48:56])
    eig_ref[8:16] = jnp.where(first, b_ref[48:56], a_ref[48:56])


def rotate(r_ref, g_ref, bo_ref, right_ref, o_ref, w_ref):
    proj = r_ref[:, 0:32, :].reshape(N * 32, 128)
    moment = jnp.dot(g_ref[...], proj, preferred_element_type=F32)
    rotated = tn(bo_ref[...], jnp.concatenate(split(moment), axis=1).astype(BF16))
    rotated = rotated[:, 128:256] + rotated[:, 0:128]
    o_ref[:, 0:8, :] = rotated[0:256].reshape(N, 8, 128)
    o_ref[:, 8:16, :] = rotated[256:512].reshape(N, 8, 128)
    pieces = r_ref[:, 32:40, :].astype(F32)
    pieces = (pieces + jnp.roll(pieces, 4, axis=1)).reshape(N // 2, 2, 8, 128)
    top = lax.broadcasted_iota(jnp.int32, (N // 2, 8, 128), 1) < 4
    left = jnp.where(top, pieces[:, 0], pieces[:, 1]).reshape(128, 128)
    right = right_ref[...]
    rows = jnp.concatenate([right, right, right, right], axis=0)
    query = lax.broadcasted_iota(jnp.int32, (32, 128), 0) // 8
    column = lax.broadcasted_iota(jnp.int32, (32, 128), 1) // 32
    rows = jnp.where(query == column, rows, 0.0)
    r1, r2 = split(rows)
    l1, l2 = split(left)
    rows = jnp.concatenate([r1, r1, r2], axis=1).astype(BF16)
    left = jnp.concatenate([l1, l2, l1], axis=0).astype(BF16)
    w_ref[...] = jnp.dot(rows, left, preferred_element_type=F32)


def column_pack(r_ref, w_ref, o_ref, s_ref):
    total = jnp.sum(r_ref[...], axis=0)
    zh = lax.axis_index("zh")
    mine = w_ref[pl.ds(pl.multiple_of(zh * 16, 16), 16)]
    o_ref[...] = jnp.broadcast_to(mine[None], (16, 16, 128))
    o_ref[2 * lax.axis_index("dp") + 1 - zh] = total
    s_ref[...] = total


def score(r_ref, s_ref, w_ref, eig_ref, d_ref, o_ref):
    zh = lax.axis_index("zh")
    partner = 2 * lax.axis_index("dp") + 1 - zh
    damped = (s_ref[...] + r_ref[partner]) / (eig_ref[...] + damping)
    d_ref[...] = jnp.where(zh == 0, damped[0:8], damped[8:16])
    local = w_ref[pl.ds(pl.multiple_of((1 - zh) * 16, 16), 16)]

    def weights(source, rows):
        return jnp.where(partner == source, local[rows], r_ref[source, rows])

    sums = []
    for q in range(16):
        rows = slice((q % 2) * 8, (q % 2) * 8 + 8)
        even = 4 * (q // 4) + (q % 4) // 2
        part = weights(even, rows) * damped[0:8] + weights(even + 2, rows) * damped[8:16]
        sums.append(jnp.sum(part, axis=0, keepdims=True))
    sums = jnp.concatenate(sums, axis=0)
    ones = jnp.ones((8, 128), F32)
    row = lax.dot_general(ones, jnp.concatenate([sums, jnp.zeros((112, 128), F32)], axis=0),
                          (((1,), (1,)), ((), ())), precision=lax.Precision.HIGHEST, preferred_element_type=F32)
    o_ref[...] = jnp.broadcast_to(row[None, 0:1], (N, 1, 128))


def last_sum(r_ref, d_ref, o_ref, e_ref):
    o_ref[...] = jnp.sum(r_ref[...], axis=0)[:, 0:16]
    e_ref[...] = d_ref[...]


def on_device(train_inputs, out_grads, basis_in, basis_out, query_left, query_right, eigenvalues):
    def shape(*dims, dtype=F32):
        return jax.ShapeDtypeStruct(dims, dtype)

    hbm = pl.BlockSpec(memory_space=pltpu.HBM)
    part = pl.pallas_call(
        partials,
        out_shape=shape(N, TAIL + 24, 128, dtype=BF16),
        in_specs=[hbm] * 5,
        scratch_shapes=[
            pltpu.VMEM((1024, 128), BF16),
            pltpu.VMEM((128, 128), BF16),
            pltpu.VMEM((128, 128), BF16),
            pltpu.VMEM((448, 256), BF16),
            pltpu.VMEM((448, 128), BF16),
            pltpu.SemaphoreType.DMA((5,)),
        ],
        compiler_params=pltpu.CompilerParams(vmem_limit_bytes=12 * 1024 * 1024),
    )(*(pltpu.with_memory_space_constraint(v, pltpu.HBM) for v in (train_inputs, basis_in, query_left, basis_out, query_right)))
    part = lax.all_to_all(part, PLANE, 0, 0, tiled=True)
    mine = call(plane_sum, shape(56, 128), part, eigenvalues.T)
    other = lax.ppermute(mine, "zh", [(0, 1), (1, 0)])
    full, right, eig = call(
        finish, (shape(N, 40, 128, dtype=BF16), shape(8, 128), shape(16, 128)), mine, other)
    full = lax.all_to_all(full, PLANE, 0, 0, tiled=True)
    rotated, weights = call(
        rotate, (shape(N, 16, 128), shape(32, 128)), full, out_grads.T, basis_out, right)
    rotated = lax.all_to_all(rotated, PLANE, 0, 0, tiled=True)
    packed, half = call(column_pack, (shape(16, 16, 128), shape(16, 128)), rotated, weights)
    packed = lax.all_to_all(packed, COLUMN, 0, 0, tiled=True)
    damped, scores = call(score, (shape(8, 128), shape(N, 1, 128)), packed, half, weights, eig)
    scores = lax.all_to_all(scores, PLANE, 0, 0, tiled=True)
    scores, damped = call(last_sum, (shape(1, 16), shape(8, 128)), scores, damped)
    return scores, damped.T[None]


def solution(mesh):
    fine = Mesh(mesh.devices.reshape(8, 2, 8, 4), ("dp", "zh", "y", "x"))
    basis = ("zh", "y", "x")
    in_specs = (
        P("dp", basis),
        P("dp", basis),
        P(basis, None),
        P(basis, None),
        P(basis, None),
        P(basis, None),
        P(None, basis),
    )
    out_specs = (P("dp", None), P("dp", None, basis))
    return jax.shard_map(
        on_device, mesh=fine, in_specs=in_specs, out_specs=out_specs, check_vma=False
    )
```
